256 devices in a mesh: video: 8 (over z), seq: 32 (over x, y, core).
Axes of the slice: x: 4, y: 4, z: 8, core: 2. Of those that a mesh axis runs over, the one named last changes fastest.
Arguments:
- queries: bfloat16 [65536, 5120], P(('video', 'seq')), parts along dimension 0, may hold values from -8 to 8
- keys: bfloat16 [65536, 5120], P(('video', 'seq')), parts along dimension 0, may hold values from -8 to 8
- values: bfloat16 [65536, 5120], P(('video', 'seq')), parts along dimension 0, may hold values from -6 to 6
- temporal_heads: int32 [4], replicated, may hold values from 0 to 39, as said below
- spatial_mask: int32 [32, 4, 4], P('seq'), may hold values 0 or 1
- temporal_mask: int32 [32, 32], replicated, may hold values 0 or 1
Outputs:
- attended: bfloat16 [65536, 5120], P(('video', 'seq')), parts along dimension 0
The draws below stay inside these ranges and needn't reach their ends.
There are 8 independent parts, one for each index of `video`. The reference program is written for one: setup_inputs(seed, part) draws one part's arguments, and reference() takes and returns one part's arrays. A program takes and returns all parts, laid end to end along the dimension named above; an argument that names none is the same for every part. Nothing has to cross between parts.
Inputs may be any that keep to these rules, and one draw needn't show every extreme that they name: `temporal_heads`: 4 different head numbers in rising order; the last one is always 40 - 1.
All inputs are finite; a program needn't handle non-finite values. No bound on the sum of `spatial_mask` on one device may be relied on, other than what follows from the above.
Results may differ from the reference program's by a relative error of at most 0.0049.
Values may be sent and summed in bfloat16 or wider, within the bound.
A program may use at most 64 MiB of HBM per device.

```python
import jax
import jax.numpy as jnp
from jax import lax

HEADS = 40
HD = 128
TEMPORAL = 4
SPATIAL = 36
TOK_DEV = 256
BLK = 64
PG = 8
NB = 4
TOKENS = 8192
N_SEQ = 32


def paired_fields(key):
    base = jax.random.fold_in(key, 11)
    first, second = jax.random.split(base, 2)
    shape = (TOKENS, HEADS * HD)
    q_field = jnp.clip(jax.random.normal(first, shape, jnp.float32), -6.0, 6.0)
    k_field = jnp.clip(jax.random.normal(second, shape, jnp.float32), -6.0, 6.0)
    return (q_field, k_field)


def draw_queries(key, part):
    return paired_fields(key)[0].astype(jnp.bfloat16)


def draw_keys(key, part):
    return paired_fields(key)[1].astype(jnp.bfloat16)


def draw_temporal_heads(key, part):
    others = jax.random.permutation(jax.random.fold_in(key, 5), HEADS - 1)[:TEMPORAL - 1]
    picked = jnp.concatenate([others.astype(jnp.int32), jnp.full((1,), HEADS - 1, jnp.int32)])
    return jnp.sort(picked).astype(jnp.int32)


def touch_ends(result, own_key, low, high):
    shape = result.shape
    index_at = [jax.random.randint(jax.random.fold_in(own_key, axis), (), 0, shape[axis]) for axis in range(len(shape))]
    result = result.at[tuple(index_at)].set(low)
    longest = shape.index(max(shape))
    index_at[longest] = (index_at[longest] + 1) % shape[longest]
    return result.at[tuple(index_at)].set(high)


def level_of(own_key, extent, cuts, smallest, top_value):
    def one(axis_at, shards_of):
        steps = jax.random.uniform(jax.random.fold_in(jax.random.fold_in(own_key, 6), axis_at), (shards_of,), jnp.float32, smallest / len(cuts), top_value / len(cuts))
        return jnp.repeat(jnp.exp(steps), extent[axis_at] // shards_of).reshape((-1,) + (1,) * (len(extent) - axis_at - 1))

    gain = one(*cuts[0])
    for cut in cuts[1:]:
        gain = gain * one(*cut)
    return gain


def normal_values(key, extent, spread, limit, shards=(), kind=jnp.bfloat16):
    factor_of = level_of(key, extent, shards, -0.22, 0.18) if shards else 1.0
    entries = jax.random.normal(key, extent, jnp.float32) * spread * factor_of
    return jnp.minimum(jnp.maximum(entries, -limit), limit).astype(kind)


def setup_inputs(seed: int = 0, part: int = 0) -> dict:
    splits = jax.random.split(jax.random.key(seed), 7)
    part_splits = jax.random.split(jax.random.fold_in(splits[6], part), 7)
    queries = draw_queries(jax.random.fold_in(jax.random.fold_in(splits[6], part), 71), part)
    keys = draw_keys(jax.random.fold_in(jax.random.fold_in(splits[6], part), 71), part)
    values = normal_values(part_splits[2], (TOKENS, HEADS * HD), 1.0, 6.0, ((0, 32),))
    temporal_heads = draw_temporal_heads(jax.random.fold_in(splits[6], 71), part)
    spatial_mask = touch_ends((jax.random.randint(splits[4], (N_SEQ, NB, NB), 0, 2) < 1).astype(jnp.int32), jax.random.fold_in(splits[4], 1), 0, 1)
    temporal_mask = touch_ends((jax.random.randint(splits[5], (N_SEQ, N_SEQ), 0, 2) < 1).astype(jnp.int32), jax.random.fold_in(splits[5], 1), 0, 1)
    return dict(queries=queries, keys=keys, values=values, temporal_heads=temporal_heads, spatial_mask=spatial_mask, temporal_mask=temporal_mask)


def attend(query, key, value, allowed):
    scores = jnp.einsum("qhd,khd->hqk", query.astype(jnp.float32), key.astype(jnp.float32)) * (HD ** -0.5)
    scores = jnp.where(allowed[None], scores, -1e30)
    top = jnp.max(scores, axis=2, keepdims=True)
    expo = jnp.exp(scores - top)
    probs = (expo / jnp.sum(expo, axis=2, keepdims=True)).astype(jnp.bfloat16)
    probs = lax.optimization_barrier(probs).astype(jnp.float32)
    mixed = jnp.einsum("hqk,khd->qhd", probs, value.astype(jnp.float32))
    return mixed.astype(jnp.bfloat16)


def reference(queries, keys, values, temporal_heads, spatial_mask, temporal_mask):
    frames = N_SEQ
    marks = jnp.any(jnp.arange(HEADS, dtype=jnp.int32)[:, None] == temporal_heads[None, :], axis=1).astype(jnp.int32)
    order = jnp.argsort(marks, stable=True).astype(jnp.int32)
    inverse = jnp.argsort(order).astype(jnp.int32)

    def arrange(array):
        return jnp.take(array.reshape(frames, TOK_DEV, HEADS, HD), order, axis=2)

    q_all, k_all, v_all = arrange(queries), arrange(keys), arrange(values)
    eye_blocks = jnp.eye(NB, dtype=bool)

    def spatial_frame(items):
        qf, kf, vf, block = items
        allow = (block != 0) | eye_blocks
        allow = jnp.broadcast_to(allow[:, None, :, None], (NB, BLK, NB, BLK)).reshape(TOK_DEV, TOK_DEV)
        return attend(qf, kf, vf, allow)

    spatial_out = lax.map(spatial_frame, (q_all[:, :, :SPATIAL], k_all[:, :, :SPATIAL], v_all[:, :, :SPATIAL], spatial_mask))

    groups = TOK_DEV // PG

    def regroup(array):
        return jnp.transpose(array[:, :, SPATIAL:].reshape(frames, groups, PG, TEMPORAL, HD), (1, 0, 2, 3, 4)).reshape(groups, frames * PG, TEMPORAL, HD)

    frame_allow = (temporal_mask != 0) | jnp.eye(frames, dtype=bool)
    frame_allow = jnp.broadcast_to(frame_allow[:, None, :, None], (frames, PG, frames, PG)).reshape(frames * PG, frames * PG)

    def temporal_group(items):
        qg, kg, vg = items
        return attend(qg, kg, vg, frame_allow)

    temporal_out = lax.map(temporal_group, (regroup(q_all), regroup(k_all), regroup(v_all)))
    temporal_out = jnp.transpose(temporal_out.reshape(groups, frames, PG, TEMPORAL, HD), (1, 0, 2, 3, 4)).reshape(frames, TOK_DEV, TEMPORAL, HD)
    joined = jnp.concatenate([spatial_out, temporal_out], axis=2)
    joined = jnp.take(joined, inverse, axis=2)
    return joined.reshape(TOKENS, HEADS * HD)
```

```python
import functools

import jax
import jax.numpy as jnp
from jax import lax
from jax.experimental import pallas as pl
from jax.experimental.pallas import tpu as pltpu
from jax.sharding import PartitionSpec as P

HEADS = 40
HD = 128
TEMPORAL = 4
BLK = 64
PG = 8
NEG = -1e30
LOG2E = 1.4426950408889634
SCALE = HD**-0.5 * LOG2E


def attend(query, key, value, bias):
    scores = lax.dot_general(
        query, key, (((1,), (1,)), ((), ())), preferred_element_type=jnp.float32
    )
    scores = scores + bias
    top = jnp.max(scores, axis=1, keepdims=True)
    expo = jnp.exp2((scores - top) * SCALE).astype(jnp.bfloat16)
    wide = jnp.concatenate([value, jnp.ones_like(value)], axis=1)
    mixed = jnp.dot(expo, wide, preferred_element_type=jnp.float32)
    return (mixed[:, :HD] / mixed[:, HD:]).astype(jnp.bfloat16)


def kernel(
    n,
    heads_hbm,
    smask_hbm,
    tmask_hbm,
    q_hbm,
    k_hbm,
    v_hbm,
    out,
    heads,
    smask,
    tmask,
    q,
    k,
    v,
    sbias,
    tbias,
    send,
    recv,
    osend,
    orecv,
    load_sem,
    small_sem,
    send_sem,
    recv_sem,
    osend_sem,
    orecv_sem,
):
    me = lax.axis_index("seq")
    tok = q.shape[1]

    def peer_of(step):
        return lax.rem(me + step, n)

    barrier = pltpu.get_barrier_semaphore()

    @pl.loop(1, n)
    def _(step):
        pl.semaphore_signal(barrier, inc=1, device_id={"seq": peer_of(step)})

    small = [
        pltpu.make_async_copy(heads_hbm, heads, small_sem.at[0]),
        pltpu.make_async_copy(smask_hbm, smask, small_sem.at[1]),
        pltpu.make_async_copy(tmask_hbm, tmask, small_sem.at[2]),
    ]
    small[0].start()
    for part, (src, dst) in enumerate(((q_hbm, q), (k_hbm, k), (v_hbm, v))):

        @pl.loop(0, HEADS)
        def _(h):
            column = pl.ds(pl.multiple_of(h * HD, HD), HD)
            pltpu.make_async_copy(src.at[:, column], dst.at[h], load_sem.at[part]).start()

    small[1].start()
    small[2].start()

    small[0].wait()
    for part, ref in enumerate((q, k, v)):
        pltpu.make_async_copy(ref, ref, load_sem.at[part]).wait()
        for i in range(TEMPORAL):
            send[i, :, part] = ref[heads[i]].reshape(n, PG, HD)

    small[1].wait()
    small[2].wait()
    blocks = tok // BLK
    for i in range(blocks):
        for j in range(blocks):
            one = jnp.float32(0.0) if i == j else jnp.where(smask[0, i, j] != 0, 0.0, NEG)
            sbias[pl.ds(i * BLK, BLK), pl.ds(j * BLK, BLK)] = jnp.full((BLK, BLK), one, jnp.float32)
    allow = (tmask[...] != 0).astype(jnp.float32)
    rows = lax.broadcasted_iota(jnp.int32, (tok, n), 0) // PG
    cols = lax.broadcasted_iota(jnp.int32, (tok, n), 1)
    spread = (rows == cols).astype(jnp.float32)
    wide = jnp.dot(spread, allow, preferred_element_type=jnp.float32)
    wide = lax.dot_general(
        wide, spread, (((1,), (1,)), ((), ())), preferred_element_type=jnp.float32
    )
    same = (
        lax.broadcasted_iota(jnp.int32, (tok, tok), 0) // PG
        == lax.broadcasted_iota(jnp.int32, (tok, tok), 1) // PG
    )
    tbias[...] = jnp.where((wide > 0.5) | same, 0.0, NEG)

    pl.semaphore_wait(barrier, n - 1)

    for i in range(TEMPORAL):

        @pl.loop(1, n)
        def _(step):
            peer = peer_of(step)
            pltpu.make_async_remote_copy(
                src_ref=send.at[i, peer],
                dst_ref=recv.at[i, me],
                send_sem=send_sem.at[i],
                recv_sem=recv_sem.at[i],
                device_id={"seq": peer},
            ).start()

        pltpu.make_async_copy(send.at[i, me], recv.at[i, me], recv_sem.at[i]).start()

    def spatial(first, last):
        @pl.loop(first, last)
        def _(h):
            column = pl.ds(pl.multiple_of(h * HD, HD), HD)
            out[:, column] = attend(q[h], k[h], v[h], sbias[...])

    cuts = (0, 20, 27, 34, 40)
    for i in range(TEMPORAL):
        spatial(cuts[i], cuts[i + 1])
        pltpu.make_async_copy(recv.at[i], recv.at[i], recv_sem.at[i]).wait()
        mixed = attend(
            recv[i, :, 0].reshape(tok, HD),
            recv[i, :, 1].reshape(tok, HD),
            recv[i, :, 2].reshape(tok, HD),
            tbias[...],
        )
        osend[i] = mixed.reshape(n, PG, HD)

        @pl.loop(1, n)
        def _(step):
            peer = peer_of(step)
            pltpu.make_async_remote_copy(
                src_ref=osend.at[i, peer],
                dst_ref=orecv.at[i, me],
                send_sem=osend_sem.at[i],
                recv_sem=orecv_sem.at[i],
                device_id={"seq": peer},
            ).start()

        pltpu.make_async_copy(osend.at[i, me], orecv.at[i, me], orecv_sem.at[i]).start()

    for i in range(TEMPORAL):
        pltpu.make_async_copy(orecv.at[i], orecv.at[i], orecv_sem.at[i]).wait()

    @pl.loop(0, HEADS)
    def _(h):
        column = pl.ds(pl.multiple_of(h * HD, HD), HD)
        slot = jnp.int32(0)
        hit = jnp.int32(0)
        for i in range(TEMPORAL):
            match = heads[i] == h
            slot = jnp.where(match, i, slot)
            hit = jnp.where(match, 1, hit)
        moved = orecv[slot].reshape(tok, HD)
        out[:, column] = jnp.where(hit != 0, moved, out[:, column])

    for i in range(TEMPORAL):
        some = pl.ds(0, n - 1)
        pltpu.make_async_copy(send.at[i, some], send.at[i, some], send_sem.at[i]).wait()
        pltpu.make_async_copy(osend.at[i, some], osend.at[i, some], osend_sem.at[i]).wait()


def on_device(queries, keys, values, temporal_heads, spatial_mask, temporal_mask):
    n = lax.axis_size("seq")
    tok, width = queries.shape
    bf16 = jnp.bfloat16
    anywhere = pl.BlockSpec(memory_space=pltpu.HBM)
    return pl.pallas_call(
        functools.partial(kernel, n),
        out_shape=jax.ShapeDtypeStruct((tok, width), bf16),
        in_specs=[anywhere] * 6,
        out_specs=pl.BlockSpec(memory_space=pltpu.VMEM),
        scratch_shapes=[
            pltpu.SMEM((TEMPORAL,), jnp.int32),
            pltpu.SMEM(spatial_mask.shape, jnp.int32),
            pltpu.VMEM(temporal_mask.shape, jnp.int32),
            pltpu.VMEM((HEADS, tok, HD), bf16),
            pltpu.VMEM((HEADS, tok, HD), bf16),
            pltpu.VMEM((HEADS, tok, HD), bf16),
            pltpu.VMEM((tok, tok), jnp.float32),
            pltpu.VMEM((tok, tok), jnp.float32),
            pltpu.VMEM((TEMPORAL, n, 3, PG, HD), bf16),
            pltpu.VMEM((TEMPORAL, n, 3, PG, HD), bf16),
            pltpu.VMEM((TEMPORAL, n, PG, HD), bf16),
            pltpu.VMEM((TEMPORAL, n, PG, HD), bf16),
            pltpu.SemaphoreType.DMA((3,)),
            pltpu.SemaphoreType.DMA((3,)),
            pltpu.SemaphoreType.DMA((TEMPORAL,)),
            pltpu.SemaphoreType.DMA((TEMPORAL,)),
            pltpu.SemaphoreType.DMA((TEMPORAL,)),
            pltpu.SemaphoreType.DMA((TEMPORAL,)),
        ],
        compiler_params=pltpu.CompilerParams(
            collective_id=0, has_side_effects=True, vmem_limit_bytes=48 << 20
        ),
    )(temporal_heads, spatial_mask, temporal_mask, queries, keys, values)


def solution(mesh):
    placed = (
        P(("video", "seq"), None),
        P(("video", "seq"), None),
        P(("video", "seq"), None),
        P(),
        P("seq", None, None),
        P(),
    )
    return jax.shard_map(
        on_device, mesh=mesh, in_specs=placed, out_specs=P(("video", "seq"), None), check_vma=False
    )
```

```python
import functools

import jax
import jax.numpy as jnp
from jax import lax
from jax.experimental import pallas as pl
from jax.experimental.pallas import tpu as pltpu
from jax.sharding import PartitionSpec as P

HEADS = 40
HD = 128
TEMPORAL = 4
BLK = 64
PG = 8
NEG = -1e30
LOG2E = 1.4426950408889634
SCALE = HD**-0.5 * LOG2E


SPATIAL = 36
UNROLL = 6
SEGMENTS = (0, 18, 24, 30, 36)
STAGES = (3, 0, 1, 2)


def score(query, key, bias):
    return (
        lax.dot_general(query, key, (((1,), (1,)), ((), ())), preferred_element_type=jnp.float32)
        + bias
    )


def weigh(scores):
    top = jnp.max(scores, axis=1, keepdims=True)
    return jnp.exp2((scores - top) * SCALE).astype(jnp.bfloat16)


def mix(expo, value):
    wide = jnp.concatenate([value, jnp.ones_like(value)], axis=1)
    mixed = jnp.dot(expo, wide, preferred_element_type=jnp.float32)
    return (mixed[:, :HD] / mixed[:, HD:]).astype(jnp.bfloat16)


def attention_kernel(
    n,
    heads_hbm,
    smask_hbm,
    tmask_hbm,
    q_hbm,
    k_hbm,
    v_hbm,
    spatial_out,
    orecv,
    heads,
    smask,
    tmask,
    q,
    k,
    v,
    sbias,
    tbias,
    scores,
    expos,
    send,
    recv,
    osend,
    first_sem,
    load_sem,
    small_sem,
    send_sem,
    recv_sem,
    osend_sem,
    orecv_sem,
):
    me = lax.axis_index("seq")
    tok = q.shape[1]

    def peer_of(step):
        return lax.rem(me + step, n)

    barrier = pltpu.get_barrier_semaphore()

    @pl.loop(1, n)
    def _(step):
        pl.semaphore_signal(barrier, inc=1, device_id={"seq": peer_of(step)})

    pairs = ((q_hbm, q), (k_hbm, k), (v_hbm, v))
    last = HEADS - 1
    first = [
        pltpu.make_async_copy(src.at[:, pl.ds(last * HD, HD)], dst.at[last], first_sem.at[part])
        for part, (src, dst) in enumerate(pairs)
    ]
    for copy in first:
        copy.start()
    small = [
        pltpu.make_async_copy(heads_hbm, heads, small_sem.at[0]),
        pltpu.make_async_copy(smask_hbm, smask, small_sem.at[1]),
        pltpu.make_async_copy(tmask_hbm, tmask, small_sem.at[2]),
    ]
    for copy in small:
        copy.start()
    for part, (src, dst) in enumerate(pairs):

        @pl.loop(0, last)
        def _(h):
            column = pl.ds(pl.multiple_of(h * HD, HD), HD)
            pltpu.make_async_copy(src.at[:, column], dst.at[h], load_sem.at[part]).start()

    for part, ref in enumerate((q, k, v)):
        first[part].wait()
        send[TEMPORAL - 1, :, part] = ref[last].reshape(n, PG, HD)

    small[1].wait()
    small[2].wait()
    blocks = tok // BLK
    for i in range(blocks):
        for j in range(blocks):
            one = jnp.float32(0.0) if i == j else jnp.where(smask[0, i, j] != 0, 0.0, NEG)
            sbias[pl.ds(i * BLK, BLK), pl.ds(j * BLK, BLK)] = jnp.full((BLK, BLK), one, jnp.float32)
    allow = (tmask[...] != 0).astype(jnp.float32)
    rows = lax.broadcasted_iota(jnp.int32, (tok, n), 0) // PG
    cols = lax.broadcasted_iota(jnp.int32, (tok, n), 1)
    spread = (rows == cols).astype(jnp.float32)
    wide = jnp.dot(spread, allow, preferred_element_type=jnp.float32)
    wide = lax.dot_general(
        wide, spread, (((1,), (1,)), ((), ())), preferred_element_type=jnp.float32
    )
    same = (
        lax.broadcasted_iota(jnp.int32, (tok, tok), 0) // PG
        == lax.broadcasted_iota(jnp.int32, (tok, tok), 1) // PG
    )
    tbias[...] = jnp.where((wide > 0.5) | same, 0.0, NEG)

    def scatter(src, dst, src_sem, dst_sem):
        @pl.loop(1, n)
        def _(step):
            peer = peer_of(step)
            pltpu.make_async_remote_copy(
                src_ref=src.at[peer],
                dst_ref=dst.at[me],
                send_sem=src_sem,
                recv_sem=dst_sem,
                device_id={"seq": peer},
            ).start()

        pltpu.make_async_copy(src.at[me], dst.at[me], dst_sem).start()

    pl.semaphore_wait(barrier, n - 1)
    for i in STAGES[:1]:
        scatter(send.at[i], recv.at[i], send_sem.at[i], recv_sem.at[i])
    small[0].wait()
    for part, ref in enumerate((q, k, v)):
        rest = ref.at[pl.ds(0, last)]
        pltpu.make_async_copy(rest, rest, load_sem.at[part]).wait()
        for i in STAGES[1:]:
            send[i, :, part] = ref[heads[i]].reshape(n, PG, HD)
    for i in STAGES[1:]:
        scatter(send.at[i], recv.at[i], send_sem.at[i], recv_sem.at[i])

    def head_of(j):
        h = jnp.minimum(j, SPATIAL - 1)
        for i in range(TEMPORAL):
            h = h + jnp.where(heads[i] <= h, 1, 0)
        return h

    def ahead(j, slot):
        h = head_of(j)
        scores[slot] = score(q[h], k[h], sbias[...])

    ahead(0, 0)
    ahead(1, 1)
    expos[0] = weigh(scores[0])

    for stage, i in enumerate(STAGES):

        @pl.loop(SEGMENTS[stage], SEGMENTS[stage + 1], step=UNROLL)
        def _(base):
            for step in range(UNROLL):
                slot = step % 2
                ahead(base + step + 2, slot)
                expos[1 - slot] = weigh(scores[1 - slot])
                spatial_out[base + step] = mix(expos[slot], v[head_of(base + step)])

        pltpu.make_async_copy(recv.at[i], recv.at[i], recv_sem.at[i]).wait()
        got = [recv[i, :, part].reshape(tok, HD) for part in range(3)]
        mixed = mix(weigh(score(got[0], got[1], tbias[...])), got[2])
        osend[i] = mixed.reshape(n, PG, HD)
        scatter(osend.at[i], orecv.at[i], osend_sem.at[i], orecv_sem.at[i])

    for i in STAGES:
        pltpu.make_async_copy(orecv.at[i], orecv.at[i], orecv_sem.at[i]).wait()
    for i in STAGES:
        some = pl.ds(0, n - 1)
        pltpu.make_async_copy(send.at[i, some], send.at[i, some], send_sem.at[i]).wait()
        pltpu.make_async_copy(osend.at[i, some], osend.at[i, some], osend_sem.at[i]).wait()


def place_kernel(heads, spatial, temporal, out, sem):
    @pl.loop(0, SPATIAL)
    def _(j):
        h = j
        for i in range(TEMPORAL):
            h = h + jnp.where(heads[i] <= h, 1, 0)
        column = pl.ds(pl.multiple_of(h * HD, HD), HD)
        pltpu.make_async_copy(spatial.at[j], out.at[:, column], sem).start()

    for i in range(TEMPORAL):
        column = pl.ds(pl.multiple_of(heads[i] * HD, HD), HD)
        pltpu.make_async_copy(temporal.at[i], out.at[:, column], sem).start()
    pltpu.make_async_copy(out, out, sem).wait()


def on_device(queries, keys, values, temporal_heads, spatial_mask, temporal_mask):
    n = lax.axis_size("seq")
    tok, width = queries.shape
    bf16 = jnp.bfloat16
    operands = (temporal_heads, spatial_mask, temporal_mask, queries, keys, values)
    in_vmem = pl.BlockSpec(memory_space=pltpu.VMEM)
    in_hbm = pl.BlockSpec(memory_space=pltpu.HBM)
    spatial, temporal = pl.pallas_call(
        functools.partial(attention_kernel, n),
        out_shape=(
            pltpu.VMEM((SPATIAL, tok, HD), bf16),
            pltpu.VMEM((TEMPORAL, n, PG, HD), bf16),
        ),
        in_specs=[in_hbm] * 6,
        out_specs=(in_vmem, in_vmem),
        scratch_shapes=[
            pltpu.SMEM((TEMPORAL,), jnp.int32),
            pltpu.SMEM(spatial_mask.shape, jnp.int32),
            pltpu.VMEM(temporal_mask.shape, jnp.int32),
            pltpu.VMEM((HEADS, tok, HD), bf16),
            pltpu.VMEM((HEADS, tok, HD), bf16),
            pltpu.VMEM((HEADS, tok, HD), bf16),
            pltpu.VMEM((tok, tok), jnp.float32),
            pltpu.VMEM((tok, tok), jnp.float32),
            pltpu.VMEM((2, tok, tok), jnp.float32),
            pltpu.VMEM((2, tok, tok), bf16),
            pltpu.VMEM((TEMPORAL, n, 3, PG, HD), bf16),
            pltpu.VMEM((TEMPORAL, n, 3, PG, HD), bf16),
            pltpu.VMEM((TEMPORAL, n, PG, HD), bf16),
            pltpu.SemaphoreType.DMA((3,)),
            pltpu.SemaphoreType.DMA((3,)),
            pltpu.SemaphoreType.DMA((3,)),
            pltpu.SemaphoreType.DMA((TEMPORAL,)),
            pltpu.SemaphoreType.DMA((TEMPORAL,)),
            pltpu.SemaphoreType.DMA((TEMPORAL,)),
            pltpu.SemaphoreType.DMA((TEMPORAL,)),
        ],
        compiler_params=pltpu.CompilerParams(
            collective_id=0, has_side_effects=True, vmem_limit_bytes=48 << 20
        ),
    )(*[pltpu.with_memory_space_constraint(x, pltpu.HBM) for x in operands])
    temporal = temporal.reshape(TEMPORAL, tok, HD)
    return pl.pallas_call(
        place_kernel,
        out_shape=jax.ShapeDtypeStruct((tok, width), bf16),
        in_specs=[pl.BlockSpec(memory_space=pltpu.SMEM), in_vmem, in_vmem],
        out_specs=in_hbm,
        scratch_shapes=[pltpu.SemaphoreType.DMA],
        compiler_params=pltpu.CompilerParams(vmem_limit_bytes=8 << 20),
    )(temporal_heads, spatial, temporal)


def solution(mesh):
    placed = (
        P(("video", "seq"), None),
        P(("video", "seq"), None),
        P(("video", "seq"), None),
        P(),
        P("seq", None, None),
        P(),
    )
    return jax.shard_map(
        on_device, mesh=mesh, in_specs=placed, out_specs=P(("video", "seq"), None), check_vma=False
    )
```

```python
import functools

import jax
import jax.numpy as jnp
from jax import lax
from jax.experimental import pallas as pl
from jax.experimental.pallas import tpu as pltpu
from jax.sharding import PartitionSpec as P

HEADS = 40
HD = 128
TEMPORAL = 4
BLK = 64
PG = 8
NEG = -1e30
LOG2E = 1.4426950408889634
SCALE = HD**-0.5 * LOG2E


SPATIAL = 36
UNROLL = 6
SEGMENTS = (0, 18, 24, 30, 36)
STAGES = (3, 0, 1, 2)
FAR = (
    (2, 2), (2, 1), (1, 2), (2, 3), (3, 2), (1, 1), (3, 3), (1, 3),
    (3, 1), (2, 0), (0, 2), (1, 0), (0, 1), (3, 0), (0, 3),
)


def score(query, key, bias):
    return (
        lax.dot_general(query, key, (((1,), (1,)), ((), ())), preferred_element_type=jnp.float32)
        + bias
    )


def weigh(scores):
    top = jnp.max(scores, axis=1, keepdims=True)
    return jnp.exp2((scores - top) * SCALE).astype(jnp.bfloat16)


def mix(expo, value):
    wide = jnp.concatenate([value, jnp.ones_like(value)], axis=1)
    mixed = jnp.dot(expo, wide, preferred_element_type=jnp.float32)
    return (mixed[:, :HD] / mixed[:, HD:]).astype(jnp.bfloat16)


def spread_head(j, heads):
    h = j
    for i in range(TEMPORAL):
        h = h + jnp.where(heads[i] - i <= j, 1, 0)
    return h


def attention_kernel(
    n,
    heads_hbm,
    smask_hbm,
    tmask_hbm,
    q_hbm,
    k_hbm,
    v_hbm,
    spatial_out,
    orecv,
    heads,
    smask,
    tmask,
    q,
    k,
    v,
    sbias,
    tbias,
    scores,
    expos,
    send,
    recv,
    osend,
    first_sem,
    load_sem,
    small_sem,
    send_sem,
    recv_sem,
    osend_sem,
    orecv_sem,
):
    me = lax.axis_index("seq")
    tok = q.shape[1]

    xs = [lax.rem(me // 8 + d, 4) * 8 for d in range(4)]
    ys = [lax.rem(lax.rem(me // 2, 4) + d, 4) * 2 for d in range(4)]
    cs = [lax.rem(me + d, 2) for d in range(2)]
    peers = [xs[dx] + ys[dy] + cs[dc] for dx, dy in FAR for dc in range(2)]
    peers.append(xs[0] + ys[0] + cs[1])

    barrier = pltpu.get_barrier_semaphore()
    for peer in peers:
        pl.semaphore_signal(barrier, inc=1, device_id={"seq": peer})

    pairs = ((q_hbm, q), (k_hbm, k), (v_hbm, v))
    last = HEADS - 1
    first = [
        pltpu.make_async_copy(src.at[:, pl.ds(last * HD, HD)], dst.at[last], first_sem.at[part])
        for part, (src, dst) in enumerate(pairs)
    ]
    for copy in first:
        copy.start()
    small = [
        pltpu.make_async_copy(heads_hbm, heads, small_sem.at[0]),
        pltpu.make_async_copy(smask_hbm, smask, small_sem.at[1]),
        pltpu.make_async_copy(tmask_hbm, tmask, small_sem.at[2]),
    ]
    for copy in small:
        copy.start()
    for part, (src, dst) in enumerate(pairs):

        @pl.loop(0, last)
        def _(h):
            column = pl.ds(pl.multiple_of(h * HD, HD), HD)
            pltpu.make_async_copy(src.at[:, column], dst.at[h], load_sem.at[part]).start()

    for part, ref in enumerate((q, k, v)):
        first[part].wait()
        send[TEMPORAL - 1, :, part] = ref[last].reshape(n, PG, HD)

    def scatter(src, dst, src_sem, dst_sem):
        for peer in peers:
            pltpu.make_async_remote_copy(
                src_ref=src.at[peer],
                dst_ref=dst.at[me],
                send_sem=src_sem,
                recv_sem=dst_sem,
                device_id={"seq": peer},
            ).start()

        pltpu.make_async_copy(src.at[me], dst.at[me], dst_sem).start()

    pl.semaphore_wait(barrier, n - 1)
    for i in STAGES[:1]:
        scatter(send.at[i], recv.at[i], send_sem.at[i], recv_sem.at[i])

    small[1].wait()
    small[2].wait()
    blocks = tok // BLK
    for i in range(blocks):
        for j in range(blocks):
            one = jnp.float32(0.0) if i == j else jnp.where(smask[0, i, j] != 0, 0.0, NEG)
            sbias[pl.ds(i * BLK, BLK), pl.ds(j * BLK, BLK)] = jnp.full((BLK, BLK), one, jnp.float32)
    allow = (tmask[...] != 0).astype(jnp.float32)
    rows = lax.broadcasted_iota(jnp.int32, (tok, n), 0) // PG
    cols = lax.broadcasted_iota(jnp.int32, (tok, n), 1)
    spread = (rows == cols).astype(jnp.float32)
    wide = jnp.dot(spread, allow, preferred_element_type=jnp.float32)
    wide = lax.dot_general(
        wide, spread, (((1,), (1,)), ((), ())), preferred_element_type=jnp.float32
    )
    same = (
        lax.broadcasted_iota(jnp.int32, (tok, tok), 0) // PG
        == lax.broadcasted_iota(jnp.int32, (tok, tok), 1) // PG
    )
    tbias[...] = jnp.where((wide > 0.5) | same, 0.0, NEG)

    small[0].wait()
    for part, ref in enumerate((q, k, v)):
        rest = ref.at[pl.ds(0, last)]
        pltpu.make_async_copy(rest, rest, load_sem.at[part]).wait()
        for i in STAGES[1:]:
            send[i, :, part] = ref[heads[i]].reshape(n, PG, HD)
    for i in STAGES[1:]:
        scatter(send.at[i], recv.at[i], send_sem.at[i], recv_sem.at[i])

    def head_of(j):
        return spread_head(jnp.minimum(j, SPATIAL - 1), heads)

    def ahead(j, slot):
        h = head_of(j)
        scores[slot] = score(q[h], k[h], sbias[...])

    ahead(0, 0)
    ahead(1, 1)
    expos[0] = weigh(scores[0])

    for stage, i in enumerate(STAGES):

        @pl.loop(SEGMENTS[stage], SEGMENTS[stage + 1], step=UNROLL)
        def _(base):
            for step in range(UNROLL):
                slot = step % 2
                ahead(base + step + 2, slot)
                expos[1 - slot] = weigh(scores[1 - slot])
                spatial_out[base + step] = mix(expos[slot], v[head_of(base + step)])

        pltpu.make_async_copy(recv.at[i], recv.at[i], recv_sem.at[i]).wait()
        got = [recv[i, :, part].reshape(tok, HD) for part in range(3)]
        mixed = mix(weigh(score(got[0], got[1], tbias[...])), got[2])
        osend[i] = mixed.reshape(n, PG, HD)
        scatter(osend.at[i], orecv.at[i], osend_sem.at[i], orecv_sem.at[i])

    for i in STAGES:
        pltpu.make_async_copy(orecv.at[i], orecv.at[i], orecv_sem.at[i]).wait()
    for i in STAGES:
        some = pl.ds(0, n - 1)
        pltpu.make_async_copy(send.at[i, some], send.at[i, some], send_sem.at[i]).wait()
        pltpu.make_async_copy(osend.at[i, some], osend.at[i, some], osend_sem.at[i]).wait()


def place_kernel(heads, spatial, temporal, out, sem):
    where = [heads[i] for i in range(TEMPORAL)]
    for j in range(SPATIAL):
        column = pl.ds(pl.multiple_of(spread_head(j, where) * HD, HD), HD)
        pltpu.make_async_copy(spatial.at[j], out.at[:, column], sem).start()
    for i in range(TEMPORAL):
        column = pl.ds(pl.multiple_of(where[i] * HD, HD), HD)
        pltpu.make_async_copy(temporal.at[i], out.at[:, column], sem).start()
    pltpu.make_async_copy(out, out, sem).wait()


def on_device(queries, keys, values, temporal_heads, spatial_mask, temporal_mask):
    n = lax.axis_size("seq")
    tok, width = queries.shape
    bf16 = jnp.bfloat16
    operands = (temporal_heads, spatial_mask, temporal_mask, queries, keys, values)
    in_vmem = pl.BlockSpec(memory_space=pltpu.VMEM)
    in_hbm = pl.BlockSpec(memory_space=pltpu.HBM)
    spatial, temporal = pl.pallas_call(
        functools.partial(attention_kernel, n),
        out_shape=(
            pltpu.VMEM((SPATIAL, tok, HD), bf16),
            pltpu.VMEM((TEMPORAL, n, PG, HD), bf16),
        ),
        in_specs=[in_hbm] * 6,
        out_specs=(in_vmem, in_vmem),
        scratch_shapes=[
            pltpu.SMEM((TEMPORAL,), jnp.int32),
            pltpu.SMEM(spatial_mask.shape, jnp.int32),
            pltpu.VMEM(temporal_mask.shape, jnp.int32),
            pltpu.VMEM((HEADS, tok, HD), bf16),
            pltpu.VMEM((HEADS, tok, HD), bf16),
            pltpu.VMEM((HEADS, tok, HD), bf16),
            pltpu.VMEM((tok, tok), jnp.float32),
            pltpu.VMEM((tok, tok), jnp.float32),
            pltpu.VMEM((2, tok, tok), jnp.float32),
            pltpu.VMEM((2, tok, tok), bf16),
            pltpu.VMEM((TEMPORAL, n, 3, PG, HD), bf16),
            pltpu.VMEM((TEMPORAL, n, 3, PG, HD), bf16),
            pltpu.VMEM((TEMPORAL, n, PG, HD), bf16),
            pltpu.SemaphoreType.DMA((3,)),
            pltpu.SemaphoreType.DMA((3,)),
            pltpu.SemaphoreType.DMA((3,)),
            pltpu.SemaphoreType.DMA((TEMPORAL,)),
            pltpu.SemaphoreType.DMA((TEMPORAL,)),
            pltpu.SemaphoreType.DMA((TEMPORAL,)),
            pltpu.SemaphoreType.DMA((TEMPORAL,)),
        ],
        compiler_params=pltpu.CompilerParams(
            collective_id=0, has_side_effects=True, vmem_limit_bytes=48 << 20
        ),
    )(*[pltpu.with_memory_space_constraint(x, pltpu.HBM) for x in operands])
    temporal = temporal.reshape(TEMPORAL, tok, HD)
    return pl.pallas_call(
        place_kernel,
        out_shape=jax.ShapeDtypeStruct((tok, width), bf16),
        in_specs=[pl.BlockSpec(memory_space=pltpu.SMEM), in_vmem, in_vmem],
        out_specs=in_hbm,
        scratch_shapes=[pltpu.SemaphoreType.DMA],
        compiler_params=pltpu.CompilerParams(vmem_limit_bytes=8 << 20),
    )(temporal_heads, spatial, temporal)


def solution(mesh):
    placed = (
        P(("video", "seq"), None),
        P(("video", "seq"), None),
        P(("video", "seq"), None),
        P(),
        P("seq", None, None),
        P(),
    )
    return jax.shard_map(
        on_device, mesh=mesh, in_specs=placed, out_specs=P(("video", "seq"), None), check_vma=False
    )
```
